256 devices in a mesh: pairs: 64 (over z_hi, x, y), slab: 4 (over z_lo, core).
Axes of the slice: x: 4, y: 4, z: 8 (z_hi: 4, z_lo: 2; z = z_hi * 2 + z_lo), core: 2. Of those that a mesh axis runs over, the one named last changes fastest.
Arguments:
- amplitudes: float32 [1024, 25600], P('pairs', 'slab'), may hold values from -6 to 6
- integrals: float32 [128, 128, 25600], P('pairs', None, 'slab'), may hold values from -0.0390625 to 0.0390625
- tile_mask: int32 [16, 400], replicated, may hold values from 0 to 1, as said below
Outputs:
- residual_sym: float32 [128, 128, 1024], P('pairs', 'slab')
The draws below stay inside these ranges and needn't reach their ends.
Inputs may be any that keep to these rules, and one draw needn't show every extreme that they name: Each row of tile_mask, split into aligned runs of 100 columns, holds in every run at least 25 and at most 75 ones; in every draw some run of some row holds exactly 75.
All inputs are finite; a program needn't handle non-finite values.
Results may differ from the reference program's by a relative error of at most 0.000086.
Values sent between devices are 32-bit elements; how exact they have to be, the bound alone decides.
No kernel may reach another device: no remote copies, remote signals or barrier semaphores. Data moves between devices by JAX's collectives and lax.ppermute only.
A program may use at most 128 MiB of HBM per device.

```python
import jax
import jax.numpy as jnp
from jax import lax

NO = 32
NV = 160
NW = 128
IJ = 1024
CD = 25600
IJT = 16
CT = 400
CT_S = 100
NZ_MAX = 75


def draw_tile_mask(key, part):
    slab_count = CT // CT_S
    count_key, spot_key, order_key = jax.random.split(key, 3)
    counts = jax.random.randint(count_key, (IJT, slab_count), CT_S // 4, NZ_MAX + 1)
    hot_spot = jax.random.randint(spot_key, (), 0, IJT * slab_count)
    flat_ids = jnp.arange(IJT * slab_count, dtype=jnp.int32).reshape(IJT, slab_count)
    counts = jnp.where(flat_ids == hot_spot, NZ_MAX, counts)
    scores = jax.random.randint(order_key, (IJT, slab_count, CT_S), 0, 1 << 20) * CT_S + jnp.arange(CT_S, dtype=jnp.int32)
    ranks = jnp.argsort(jnp.argsort(scores, axis=2), axis=2)
    return (ranks < counts[:, :, None]).astype(jnp.int32).reshape(IJT, CT)


def shard_levels(stream_key, extent, shards, smallest, high):
    def one(dim, parts):
        heights = jax.random.uniform(jax.random.fold_in(jax.random.fold_in(stream_key, 6), dim), (parts,), jnp.float32, smallest / len(shards), high / len(shards))
        return jnp.repeat(jnp.exp(heights), extent[dim] // parts).reshape((-1,) + (1,) * (len(extent) - dim - 1))

    level = one(*shards[0])
    for cut in shards[1:]:
        level = level * one(*cut)
    return level


def normal_values(rng, shape, scale, bound, pieces=(), kind=jnp.bfloat16):
    result = jax.random.normal(rng, shape, jnp.float32) * scale
    if len(pieces) > 0:
        result = shard_levels(rng, shape, pieces, -0.22, 0.18) * result
    return jnp.clip(result, min=-bound, max=bound).astype(kind)


def setup_inputs(seed: int = 0) -> dict:
    arg_keys = jax.random.split(jax.random.key(seed), 4)
    return {
        "amplitudes": normal_values(arg_keys[0], (IJ, CD), 1.0, 6.0, ((0, 64), (1, 4)), jnp.float32),
        "integrals": normal_values(arg_keys[1], (NW, NW, CD), CD ** -0.5, 0.0390625, ((0, 64), (2, 4)), jnp.float32),
        "tile_mask": draw_tile_mask(jax.random.fold_in(arg_keys[3], 71), 0),
    }


def reference(amplitudes, integrals, tile_mask):
    expanded = jnp.repeat(jnp.repeat(tile_mask.astype(jnp.float32), 64, axis=0), 64, axis=1)
    masked = amplitudes * expanded
    flat_ints = integrals.reshape(NW * NW, NV * NV)
    ladder = lax.dot_general(flat_ints, masked, (((1,), (1,)), ((), ())), precision=lax.Precision.HIGHEST, preferred_element_type=jnp.float32)
    ladder = ladder.reshape(NW, NW, NO, NO)
    residual_sym = ladder + ladder.transpose(1, 0, 3, 2)
    return residual_sym.reshape(NW, NW, NO * NO)
```

```python
import functools

import jax
import jax.numpy as jnp
from jax import lax
from jax.experimental import pallas as pl
from jax.experimental.pallas import tpu as pltpu
from jax.sharding import PartitionSpec as P


NO = 32
TILE = 64
SLOTS = 75
HALF = 38
KC = 1280
AX = ("pairs", "slab")
OFFS = (0, 3, 1, 2)


def device(z, x, y, s):
    return ((z % 4) * 16 + (x % 4) * 4 + (y % 4)) * 4 + s


def perm(f):
    return [
        (device(z, x, y, s), device(*f(z, x, y, s)))
        for z in range(4) for x in range(4) for y in range(4) for s in range(4)
    ]


SHIFT = {
    "z": [perm(lambda z, x, y, s: (z + 1, x, y, s)), perm(lambda z, x, y, s: (z - 1, x, y, s))],
    "x": [perm(lambda z, x, y, s: (z, x + 1, y, s)), perm(lambda z, x, y, s: (z, x - 1, y, s))],
    "y": [perm(lambda z, x, y, s: (z, x, y + 1, s)), perm(lambda z, x, y, s: (z, x, y - 1, s))],
}
OTHER_CORE = perm(lambda z, x, y, s: (z, x, y, s ^ 1))
OTHER_Z_LO = perm(lambda z, x, y, s: (z, x, y, s ^ 2))
MIRROR_X = [perm(lambda z, x, y, s, d=d: (s, x + d, y, z)) for d in range(4)]
MIRROR_Y = [perm(lambda z, x, y, s, d=d: (z, x, y + d, s)) for d in range(4)]

SMEM = pl.BlockSpec(memory_space=pltpu.SMEM)
VMEM = pl.BlockSpec(memory_space=pltpu.VMEM)


def f32(*shape):
    return jax.ShapeDtypeStruct(shape, jnp.float32)


def low_lanes(rows):
    return lax.broadcasted_iota(jnp.int32, (rows, 128), 1) < 64


def pack_kernel(mask_ref, coord_ref, amp_ref, out_ref, buf_ref):
    z, x, s = coord_ref[0], coord_ref[1], coord_ref[3]
    t = z * 4 + x
    low = low_lanes(8)
    count = jnp.int32(0)
    for g in range(50):
        r0 = amp_ref[0:8, g * 128:(g + 1) * 128]
        r1 = amp_ref[8:16, g * 128:(g + 1) * 128]
        buf_ref[count] = jnp.where(low, r0, pltpu.roll(r1, 64, 1))
        count = count + mask_ref[t, s * 100 + 2 * g]
        buf_ref[count] = jnp.where(low, pltpu.roll(r0, 64, 1), r1)
        count = count + mask_ref[t, s * 100 + 2 * g + 1]
    out_ref[...] = buf_ref[0:SLOTS]


def pack(tile_mask, coords, amplitudes):
    return pl.pallas_call(
        pack_kernel,
        out_shape=f32(SLOTS, 8, 128),
        in_specs=[SMEM, SMEM, VMEM],
        out_specs=VMEM,
        scratch_shapes=[pltpu.VMEM((SLOTS + 1, 8, 128), jnp.float32)],
        name="pack",
    )(tile_mask, coords, amplitudes)


def split_kernel(coord_ref, v_ref, hi_ref, lo_ref, buf_ref):
    s = coord_ref[3]
    for cc in range(2):
        for zz in range(2):
            block = pl.multiple_of((s ^ (zz * 2 + cc)) * 32, 32)
            for a in range(2):
                for g in range(KC // 128):
                    lanes = slice(g * 128, (g + 1) * 128)
                    buf_ref[g, pl.ds(cc * 128 + zz * 64 + a, 32, stride=2), :] = v_ref[a, pl.ds(block, 32), lanes]
    for g in range(KC // 128):
        lanes = slice(g * 128, (g + 1) * 128)
        v = buf_ref[g]
        hi = v.astype(jnp.bfloat16)
        hi_ref[:, lanes] = hi
        lo_ref[:, lanes] = (v - hi.astype(jnp.float32)).astype(jnp.bfloat16)


def split(coords, integrals):
    bf = jax.ShapeDtypeStruct((256, 6400), jnp.bfloat16)
    return pl.pallas_call(
        split_kernel,
        out_shape=(bf, bf),
        grid=(6400 // KC,),
        in_specs=[SMEM, pl.BlockSpec((2, 128, KC), lambda k: (0, 0, k))],
        out_specs=[pl.BlockSpec((256, KC), lambda k: (0, k))] * 2,
        scratch_shapes=[pltpu.VMEM((KC // 128, 256, 128), jnp.float32)],
        name="split",
    )(coords, integrals)


def ladder_kernel(x_first, slot_ref, rows_ref, own, fwd, bwd, far0, far1, vhi_ref, vlo_ref, keep_ref, send_ref, ehi, elo, acc):
    step = pl.program_id(0)
    low = low_lanes(8)
    groups = KC // 128
    for a in range(4):
        t = rows_ref[a]
        for g in range(groups):
            s0 = slot_ref[t, step * (2 * groups) + 2 * g]
            s1 = slot_ref[t, step * (2 * groups) + 2 * g + 1]
            k0 = jnp.maximum(s0, 0)
            k1 = jnp.maximum(s1, 0)
            for b in range(4):
                outer, inner = (b, a) if x_first else (a, b)
                ref = (own, fwd, bwd, far0 if inner < 2 else far1)[outer]
                i = inner % 2 if outer == 3 else inner
                v0 = jnp.where(s0 >= 0, ref[i, k0], 0.0)
                v1 = jnp.where(s1 >= 0, ref[i, k1], 0.0)
                r0 = jnp.where(low, v0, pltpu.roll(v1, 64, 1))
                r1 = jnp.where(low, pltpu.roll(v0, 64, 1), v1)
                v = jnp.concatenate([r0, r1], axis=0)
                hi = v.astype(jnp.bfloat16)
                row = (a * 4 + b) * 16
                ehi[row:row + 16, g * 128:(g + 1) * 128] = hi
                elo[row:row + 16, g * 128:(g + 1) * 128] = (v - hi.astype(jnp.float32)).astype(jnp.bfloat16)
    dot = functools.partial(
        lax.dot_general, dimension_numbers=(((1,), (1,)), ((), ())), preferred_element_type=jnp.float32
    )
    vhi = vhi_ref[...]
    part = dot(elo[...], vhi) + dot(ehi[...], vlo_ref[...]) + dot(ehi[...], vhi)

    @pl.when(step == 0)
    def _():
        acc[...] = part

    @pl.when(step > 0)
    def _():
        acc[...] += part

    @pl.when(step == pl.num_programs(0) - 1)
    def _():
        keep_ref[...] = acc[:, 0:128]
        send_ref[...] = acc[:, 128:256]


def ladder(x_first, slots, rows, parts, vhi, vlo):
    whole = [pl.BlockSpec(p.shape, lambda k: (0, 0, 0, 0), pipeline_mode=pl.Buffered(1)) for p in parts]
    return pl.pallas_call(
        functools.partial(ladder_kernel, x_first),
        out_shape=(f32(256, 128), f32(256, 128)),
        grid=(6400 // KC,),
        in_specs=[SMEM, SMEM] + whole + [pl.BlockSpec((256, KC), lambda k: (0, k))] * 2,
        out_specs=[pl.BlockSpec((256, 128), lambda k: (0, 0))] * 2,
        scratch_shapes=[
            pltpu.VMEM((256, KC), jnp.bfloat16),
            pltpu.VMEM((256, KC), jnp.bfloat16),
            pltpu.VMEM((256, 256), jnp.float32),
        ],
        name="ladder_x" if x_first else "ladder_y",
    )(slots, rows, *parts, vhi, vlo)


def halves_kernel(q0, r0, q1, r1, keep_ref, send_ref):
    low = low_lanes(256)
    a = q0[...] + r0[...]
    b = q1[...] + r1[...]
    keep_ref[...] = jnp.where(low, a, pltpu.roll(b, 64, 1))
    send_ref[...] = jnp.where(low, pltpu.roll(a, 64, 1), b)


def halves(q0, r0, q1, r1):
    return pl.pallas_call(
        halves_kernel, out_shape=(f32(256, 128), f32(256, 128)), in_specs=[VMEM] * 4, out_specs=[VMEM] * 2, name="halves"
    )(q0, r0, q1, r1)


def mirror_kernel(coord_ref, k0, r0, k1, r1, own_ref, s0, s1, s2, s3, lc, mc, mt, blocks):
    z, x, y = coord_ref[0], coord_ref[1], coord_ref[2]
    for j, (kr, rr) in enumerate(((k0, r0), (k1, r1))):
        for a in range(4):
            for b in range(4):
                row = (a * 4 + b) * 16
                v = kr[row:row + 16, :] + rr[row:row + 16, :]
                place = ((x + OFFS[a]) & 3) * 64 + ((y + OFFS[b]) & 3) * 16
                lc[pl.ds(pl.multiple_of(((z + OFFS[2 * j]) & 3) * 256 + place, 16), 16), :] = v
                lc[pl.ds(pl.multiple_of(((z + OFFS[2 * j + 1]) & 3) * 256 + place, 16), 16), :] = pltpu.roll(v, 64, 1)
    for i in range(NO):
        mc[i * NO:(i + 1) * NO, :] = lc[pl.ds(i, NO, stride=NO), :]
    own_ref[...] = jnp.transpose(lc[...])[0:64, :]
    mt[...] = jnp.transpose(mc[...])[0:64, :]
    for q in range(16):
        for e in range(2):
            for bb in range(2):
                blocks[q, 2 * e + bb:2 * e + bb + 1, :] = mt[4 * q + 2 * bb + e:4 * q + 2 * bb + e + 1, :]
    for dx, out in enumerate((s0, s1, s2, s3)):
        for dy in range(4):
            q = ((x + dx) & 3) * 4 + ((y + dy) & 3)
            out[dy * 4:dy * 4 + 4, :] = blocks[q, 0:4, :]


def mirror(coords, k0, r0, k1, r1):
    return pl.pallas_call(
        mirror_kernel,
        out_shape=(f32(64, 1024),) + (f32(16, 1024),) * 4,
        in_specs=[SMEM] + [VMEM] * 4,
        out_specs=[VMEM] * 5,
        scratch_shapes=[
            pltpu.VMEM((1024, 128), jnp.float32),
            pltpu.VMEM((1024, 128), jnp.float32),
            pltpu.VMEM((64, 1024), jnp.float32),
            pltpu.VMEM((16, 8, 1024), jnp.float32),
        ],
        name="mirror",
    )(coords, k0, r0, k1, r1)


def regroup_kernel(i0, i1, i2, i3, o0, o1, o2, o3):
    for dy, out in enumerate((o0, o1, o2, o3)):
        for dx, ref in enumerate((i0, i1, i2, i3)):
            out[dx * 4:dx * 4 + 4, :] = ref[dy * 4:dy * 4 + 4, :]


def regroup(parts):
    return pl.pallas_call(
        regroup_kernel, out_shape=(f32(16, 1024),) * 4, in_specs=[VMEM] * 4, out_specs=[VMEM] * 4, name="regroup"
    )(*parts)


def finish_kernel(coord_ref, own, i0, i1, i2, i3, out_ref, blocks, total):
    x, y = coord_ref[1], coord_ref[2]
    for dy, ref in enumerate((i0, i1, i2, i3)):
        for dx in range(4):
            q = ((x - dx) & 3) * 4 + ((y - dy) & 3)
            blocks[q, 0:4, :] = ref[dx * 4:dx * 4 + 4, :]
    for g in range(8):
        lanes = slice(g * 128, (g + 1) * 128)
        for q in range(16):
            total[g, q * 4:q * 4 + 4, :] = own[q * 4:q * 4 + 4, lanes] + blocks[q, 0:4, lanes]
        for a in range(2):
            out_ref[a, :, lanes] = total[g, pl.ds(a, 32, stride=2), :]


def finish(coords, own, parts):
    return pl.pallas_call(
        finish_kernel,
        out_shape=f32(2, 32, 1024),
        in_specs=[SMEM] + [VMEM] * 5,
        out_specs=VMEM,
        scratch_shapes=[pltpu.VMEM((16, 8, 1024), jnp.float32), pltpu.VMEM((8, 64, 128), jnp.float32)],
        name="finish",
    )(coords, own, *parts)


def ring(axis, own, cut):
    up, down = SHIFT[axis]
    fwd = lax.ppermute(own, AX, up)
    bwd = lax.ppermute(own, AX, down)
    far0 = lax.ppermute(fwd[:cut], AX, up)
    far1 = lax.ppermute(bwd[cut:], AX, down)
    return fwd, bwd, far0, far1


def shards(amplitudes, integrals, tile_mask):
    pair = lax.axis_index("pairs").astype(jnp.int32)
    slab = lax.axis_index("slab").astype(jnp.int32)
    z, x, y = pair // 16, (pair // 4) % 4, pair % 4
    coords = jnp.stack([z, x, y, slab])
    mask = lax.dynamic_slice_in_dim(tile_mask, slab * 100, 100, 1)
    before = jnp.cumsum(mask, axis=1) - mask
    slots = jnp.where(mask != 0, before, -1)

    own = pack(tile_mask, coords, amplitudes)
    vhi, vlo = split(coords, integrals)
    fwd, bwd, far0, far1 = ring("z", own, HALF)
    chunks = [own, fwd, bwd, jnp.concatenate([far0, far1])]
    results = []
    for k, chunk in enumerate(chunks):
        x_first = k % 2 == 0
        first, second = ("x", "y") if x_first else ("y", "x")
        p, m, h0, h1 = ring(first, chunk, HALF)
        line = jnp.stack([chunk, p, m, jnp.concatenate([h0, h1])])
        parts = (line,) + ring(second, line, 2)
        rows = ((z + OFFS[k]) % 4) * 4 + (x + jnp.array(OFFS, jnp.int32)) % 4
        keep, send = ladder(x_first, slots, rows, parts, vhi, vlo)
        results.append((keep, lax.ppermute(send, AX, OTHER_CORE)))
    sums = []
    for k in (0, 2):
        keep, send = halves(*results[k], *results[k + 1])
        sums += [keep, lax.ppermute(send, AX, OTHER_Z_LO)]
    mine, *blocks = mirror(coords, *sums)
    blocks = regroup([lax.ppermute(b, AX, MIRROR_X[d]) for d, b in enumerate(blocks)])
    blocks = [blocks[0]] + [lax.ppermute(blocks[d], AX, MIRROR_Y[d]) for d in range(1, 4)]
    return finish(coords, mine, blocks)


def solution(mesh):
    return jax.shard_map(
        shards,
        mesh=mesh,
        in_specs=(P("pairs", "slab"), P("pairs", None, "slab"), P()),
        out_specs=P("pairs", "slab", None),
        check_vma=False,
    )
```

```python
import functools

import jax
import jax.numpy as jnp
from jax import lax
from jax.experimental import pallas as pl
from jax.experimental.pallas import tpu as pltpu
from jax.sharding import PartitionSpec as P


NO = 32
SLOTS = 75
KC = 640
SPLIT = 1280
AX = ("pairs", "slab")
XOR = (0, 1, 3, 2)


def device(z, x, y, s):
    return ((z % 4) * 16 + (x % 4) * 4 + (y % 4)) * 4 + s


def perm(f):
    return [
        (device(z, x, y, s), device(*f(z, x, y, s)))
        for z in range(4) for x in range(4) for y in range(4) for s in range(4)
    ]


SWAP = {
    "z": {d: perm(lambda z, x, y, s, d=d: (z ^ d, x, y, s)) for d in (1, 2, 3)},
    "x": {d: perm(lambda z, x, y, s, d=d: (z, x ^ d, y, s)) for d in (1, 3)},
    "y": {d: perm(lambda z, x, y, s, d=d: (z, x, y ^ d, s)) for d in (1, 3)},
}
OTHER_CORE = perm(lambda z, x, y, s: (z, x, y, s ^ 1))
OTHER_Z_LO = perm(lambda z, x, y, s: (z, x, y, s ^ 2))
MIRROR_X = [perm(lambda z, x, y, s, d=d: (s, x + d, y, z)) for d in range(4)]
MIRROR_Y = [perm(lambda z, x, y, s, d=d: (z, x, y + d, s)) for d in range(4)]

SMEM = pl.BlockSpec(memory_space=pltpu.SMEM)
VMEM = pl.BlockSpec(memory_space=pltpu.VMEM)


def f32(*shape):
    return jax.ShapeDtypeStruct(shape, jnp.float32)


def low_lanes(rows):
    return lax.broadcasted_iota(jnp.int32, (rows, 128), 1) < 64


def pack_kernel(mask_ref, coord_ref, amp_ref, out_ref, buf_ref):
    z, x, s = coord_ref[0], coord_ref[1], coord_ref[3]
    t = z * 4 + x
    low = low_lanes(8)
    count = jnp.int32(0)
    for g in range(50):
        r0 = amp_ref[0:8, g * 128:(g + 1) * 128]
        r1 = amp_ref[8:16, g * 128:(g + 1) * 128]
        buf_ref[count] = jnp.where(low, r0, pltpu.roll(r1, 64, 1))
        count = count + mask_ref[t, s * 100 + 2 * g]
        buf_ref[count] = jnp.where(low, pltpu.roll(r0, 64, 1), r1)
        count = count + mask_ref[t, s * 100 + 2 * g + 1]
    out_ref[...] = buf_ref[0:SLOTS]


def pack(tile_mask, coords, amplitudes):
    return pl.pallas_call(
        pack_kernel,
        out_shape=f32(SLOTS, 8, 128),
        in_specs=[SMEM, SMEM, VMEM],
        out_specs=VMEM,
        scratch_shapes=[pltpu.VMEM((SLOTS + 1, 8, 128), jnp.float32)],
        compiler_params=pltpu.CompilerParams(vmem_limit_bytes=6 << 20),
        name="pack",
    )(tile_mask, coords, amplitudes)


def split_kernel(coord_ref, v_ref, hi_ref, lo_ref, buf_ref):
    s = coord_ref[3]
    for cc in range(2):
        for zz in range(2):
            block = pl.multiple_of((s ^ (zz * 2 + cc)) * 32, 32)
            for a in range(2):
                for g in range(SPLIT // 128):
                    lanes = slice(g * 128, (g + 1) * 128)
                    buf_ref[g, pl.ds(cc * 128 + zz * 64 + a, 32, stride=2), :] = v_ref[a, pl.ds(block, 32), lanes]
    for g in range(SPLIT // 128):
        lanes = slice(g * 128, (g + 1) * 128)
        v = buf_ref[g]
        hi = v.astype(jnp.bfloat16)
        hi_ref[:, lanes] = hi
        lo_ref[:, lanes] = (v - hi.astype(jnp.float32)).astype(jnp.bfloat16)


def split(coords, integrals):
    bf = jax.ShapeDtypeStruct((256, 6400), jnp.bfloat16)
    return pl.pallas_call(
        split_kernel,
        out_shape=(bf, bf),
        grid=(6400 // SPLIT,),
        in_specs=[SMEM, pl.BlockSpec((2, 128, SPLIT), lambda k: (0, 0, k))],
        out_specs=[pl.BlockSpec((256, SPLIT), lambda k: (0, k))] * 2,
        scratch_shapes=[pltpu.VMEM((SPLIT // 128, 256, 128), jnp.float32)],
        cost_estimate=pl.CostEstimate(flops=8 * 256 * 6400, bytes_accessed=4 * 256 * 6400 * 2, transcendentals=0),
        compiler_params=pltpu.CompilerParams(vmem_limit_bytes=12 << 20),
        name="split",
    )(coords, integrals)


def ladder_kernel(
    x_first, slot_ref, rows_ref, own, first, second, q1, q2, q3, vhi_ref, vlo_ref,
    keep_ref, send_ref, hi0, lo0, hi1, lo1, acc,
):
    low = low_lanes(8)
    groups = KC // 128

    def unpack(step, ehi, elo):
        for a in range(4):
            t = rows_ref[a]
            for g in range(groups):
                s0 = slot_ref[t, step * (2 * groups) + 2 * g]
                s1 = slot_ref[t, step * (2 * groups) + 2 * g + 1]
                k0 = jnp.maximum(s0, 0)
                k1 = jnp.maximum(s1, 0)
                for b in range(4):
                    i, j = (a, b) if x_first else (b, a)
                    if i == 0:
                        src = own if j == 0 else second.at[j - 1]
                    else:
                        src = (first, q1, q2, q3)[j].at[i - 1]
                    v0 = jnp.where(s0 >= 0, src[k0], 0.0)
                    v1 = jnp.where(s1 >= 0, src[k1], 0.0)
                    r0 = jnp.where(low, v0, pltpu.roll(v1, 64, 1))
                    r1 = jnp.where(low, pltpu.roll(v0, 64, 1), v1)
                    v = jnp.concatenate([r0, r1], axis=0)
                    hi = v.astype(jnp.bfloat16)
                    row = (a * 4 + b) * 16
                    ehi[row:row + 16, g * 128:(g + 1) * 128] = hi
                    elo[row:row + 16, g * 128:(g + 1) * 128] = (v - hi.astype(jnp.float32)).astype(jnp.bfloat16)

    def multiply(step, ehi, elo):
        dot = functools.partial(
            lax.dot_general, dimension_numbers=(((1,), (1,)), ((), ())), preferred_element_type=jnp.float32
        )
        lanes = pl.ds(pl.multiple_of(step * KC, KC), KC)
        vhi = vhi_ref[:, lanes]
        acc[...] += dot(elo[...], vhi) + dot(ehi[...], vlo_ref[:, lanes]) + dot(ehi[...], vhi)

    acc[...] = jnp.zeros_like(acc)
    hi1[...] = jnp.zeros_like(hi1)
    lo1[...] = jnp.zeros_like(lo1)

    def two_steps(m, carry):
        multiply(jnp.maximum(2 * m - 1, 0), hi1, lo1)
        unpack(2 * m, hi0, lo0)
        multiply(2 * m, hi0, lo0)
        unpack(2 * m + 1, hi1, lo1)
        return carry

    lax.fori_loop(0, 3200 // KC, two_steps, 0)
    multiply(6400 // KC - 1, hi1, lo1)
    keep_ref[...] = acc[:, 0:128]
    send_ref[...] = acc[:, 128:256]


def ladder(x_first, slots, rows, parts, vhi, vlo):
    return pl.pallas_call(
        functools.partial(ladder_kernel, x_first),
        out_shape=(f32(256, 128), f32(256, 128)),
        in_specs=[SMEM, SMEM] + [VMEM] * (len(parts) + 2),
        out_specs=[VMEM] * 2,
        scratch_shapes=[pltpu.VMEM((256, KC), jnp.bfloat16)] * 4 + [pltpu.VMEM((256, 256), jnp.float32)],
        cost_estimate=pl.CostEstimate(flops=6 * 256 * 256 * 6400, bytes_accessed=12 * 1024 * 1024, transcendentals=0),
        compiler_params=pltpu.CompilerParams(vmem_limit_bytes=8 << 20),
        name="ladder_x" if x_first else "ladder_y",
    )(slots, rows, *parts, vhi, vlo)


def halves_kernel(q0, r0, q1, r1, keep_ref, send_ref):
    low = low_lanes(256)
    a = q0[...] + r0[...]
    b = q1[...] + r1[...]
    keep_ref[...] = jnp.where(low, a, pltpu.roll(b, 64, 1))
    send_ref[...] = jnp.where(low, pltpu.roll(a, 64, 1), b)


def halves(q0, r0, q1, r1):
    return pl.pallas_call(
        halves_kernel, out_shape=(f32(256, 128), f32(256, 128)), in_specs=[VMEM] * 4, out_specs=[VMEM] * 2, name="halves",
        compiler_params=pltpu.CompilerParams(vmem_limit_bytes=6 << 20),
    )(q0, r0, q1, r1)


def mirror_kernel(coord_ref, k0, r0, k1, r1, own_ref, s0, s1, s2, s3, lc, mc, mt, blocks):
    z, x, y = coord_ref[0], coord_ref[1], coord_ref[2]
    for j, (kr, rr) in enumerate(((k0, r0), (k1, r1))):
        for a in range(4):
            for b in range(4):
                row = (a * 4 + b) * 16
                v = kr[row:row + 16, :] + rr[row:row + 16, :]
                place = (x ^ XOR[a]) * 64 + (y ^ XOR[b]) * 16
                lc[pl.ds(pl.multiple_of((z ^ XOR[2 * j]) * 256 + place, 16), 16), :] = v
                lc[pl.ds(pl.multiple_of((z ^ XOR[2 * j + 1]) * 256 + place, 16), 16), :] = pltpu.roll(v, 64, 1)
    for i in range(NO):
        mc[i * NO:(i + 1) * NO, :] = lc[pl.ds(i, NO, stride=NO), :]
    own_ref[...] = jnp.transpose(lc[...])[0:64, :]
    mt[...] = jnp.transpose(mc[...])[0:64, :]
    for q in range(16):
        for e in range(2):
            for bb in range(2):
                blocks[q, 2 * e + bb:2 * e + bb + 1, :] = mt[4 * q + 2 * bb + e:4 * q + 2 * bb + e + 1, :]
    for dx, out in enumerate((s0, s1, s2, s3)):
        for dy in range(4):
            q = ((x + dx) & 3) * 4 + ((y + dy) & 3)
            out[dy * 4:dy * 4 + 4, :] = blocks[q, 0:4, :]


def mirror(coords, k0, r0, k1, r1):
    return pl.pallas_call(
        mirror_kernel,
        out_shape=(f32(64, 1024),) + (f32(16, 1024),) * 4,
        in_specs=[SMEM] + [VMEM] * 4,
        out_specs=[VMEM] * 5,
        scratch_shapes=[
            pltpu.VMEM((1024, 128), jnp.float32),
            pltpu.VMEM((1024, 128), jnp.float32),
            pltpu.VMEM((64, 1024), jnp.float32),
            pltpu.VMEM((16, 8, 1024), jnp.float32),
        ],
        compiler_params=pltpu.CompilerParams(vmem_limit_bytes=8 << 20),
        name="mirror",
    )(coords, k0, r0, k1, r1)


def regroup_kernel(i0, i1, i2, i3, o0, o1, o2, o3):
    for dy, out in enumerate((o0, o1, o2, o3)):
        for dx, ref in enumerate((i0, i1, i2, i3)):
            out[dx * 4:dx * 4 + 4, :] = ref[dy * 4:dy * 4 + 4, :]


def regroup(parts):
    return pl.pallas_call(
        regroup_kernel, out_shape=(f32(16, 1024),) * 4, in_specs=[VMEM] * 4, out_specs=[VMEM] * 4, name="regroup",
        compiler_params=pltpu.CompilerParams(vmem_limit_bytes=4 << 20),
    )(*parts)


def finish_kernel(coord_ref, own, i0, i1, i2, i3, out_ref, blocks, total):
    x, y = coord_ref[1], coord_ref[2]
    for dy, ref in enumerate((i0, i1, i2, i3)):
        for dx in range(4):
            q = ((x - dx) & 3) * 4 + ((y - dy) & 3)
            blocks[q, 0:4, :] = ref[dx * 4:dx * 4 + 4, :]
    for g in range(8):
        lanes = slice(g * 128, (g + 1) * 128)
        for q in range(16):
            total[g, q * 4:q * 4 + 4, :] = own[q * 4:q * 4 + 4, lanes] + blocks[q, 0:4, lanes]
        for a in range(2):
            out_ref[a, :, lanes] = total[g, pl.ds(a, 32, stride=2), :]


def finish(coords, own, parts):
    return pl.pallas_call(
        finish_kernel,
        out_shape=f32(2, 32, 1024),
        in_specs=[SMEM] + [VMEM] * 5,
        out_specs=VMEM,
        scratch_shapes=[pltpu.VMEM((16, 8, 1024), jnp.float32), pltpu.VMEM((8, 64, 128), jnp.float32)],
        compiler_params=pltpu.CompilerParams(vmem_limit_bytes=6 << 20),
        name="finish",
    )(coords, own, *parts)


def send(value, table):
    return lax.ppermute(value, AX, table)


def ring(axis, own, light, heavy):
    near = {d: send(own, SWAP[axis][d]) for d in (light, heavy)}
    return near[1], near[3], send(near[light], SWAP[axis][heavy])


def steps(amplitudes, integrals, tile_mask):
    pair = lax.axis_index("pairs").astype(jnp.int32)
    slab = lax.axis_index("slab").astype(jnp.int32)
    z, x, y = pair // 16, (pair // 4) % 4, pair % 4
    coords = jnp.stack([z, x, y, slab])
    mask = lax.dynamic_slice_in_dim(tile_mask, slab * 100, 100, 1)
    before = jnp.cumsum(mask, axis=1) - mask
    slots = jnp.where(mask != 0, before, -1)

    own = pack(tile_mask, coords, amplitudes)
    vhi, vlo = split(coords, integrals)
    chunks = (own,) + tuple(send(own, SWAP["z"][d]) for d in (1, 3, 2))
    orders = ((1, 3), (1, 3), (3, 1), (3, 1))
    firsts = [jnp.stack(ring("xy"[k % 2], chunks[k], *orders[k])) for k in range(4)]
    column = jnp.stack(ring("y", own, 1, 3))
    line = firsts[0]
    seconds = (column,) + tuple(send(column if d == 3 else line, SWAP["z"][d]) for d in (1, 3, 2))
    results = []
    for k in range(4):
        cross = ring("yx"[k % 2], firsts[k], *orders[k])
        rows = (z ^ XOR[k]) * 4 + (x ^ jnp.array(XOR, jnp.int32))
        keep, away = ladder(k % 2 == 0, slots, rows, (chunks[k], firsts[k], seconds[k]) + cross, vhi, vlo)
        results.append((keep, send(away, OTHER_CORE)))
    sums = []
    for k in (0, 2):
        keep, away = halves(*results[k], *results[k + 1])
        sums += [keep, send(away, OTHER_Z_LO)]
    mine, *blocks = mirror(coords, *sums)
    blocks = regroup([lax.ppermute(b, AX, MIRROR_X[d]) for d, b in enumerate(blocks)])
    blocks = [blocks[0]] + [lax.ppermute(blocks[d], AX, MIRROR_Y[d]) for d in range(1, 4)]
    return finish(coords, mine, blocks)


def solution(mesh):
    return jax.shard_map(
        steps,
        mesh=mesh,
        in_specs=(P("pairs", "slab"), P("pairs", None, "slab"), P()),
        out_specs=P("pairs", "slab", None),
        check_vma=False,
    )
```
